32 devices in a mesh: pipe: 4 (over z), ctx: 8 (over y, x, core).
Axes of the slice: x: 2, y: 2, z: 4, core: 2. Of those that a mesh axis runs over, the one named last changes fastest.
Arguments:
- queries: bfloat16 [4, 2048, 2048], P('pipe', 'ctx'), may hold values from -120 to 120
- keys: bfloat16 [4, 2048, 512], P('pipe', 'ctx'), may hold values from -6.5 to 6.5
- values: bfloat16 [4, 2048, 512], P('pipe', 'ctx'), may hold values from -24 to 24
- out_weight: bfloat16 [4, 2048, 4096], P('pipe'), may hold values from -0.125 to 0.125
Outputs:
- handed: bfloat16 [4, 2048, 4096], P('pipe', 'ctx')
The draws below stay inside these ranges and needn't reach their ends.
All inputs are finite; a program needn't handle non-finite values.
Results may differ from the reference program's by a relative error of at most 0.0065.
Values may be sent and summed in bfloat16 or wider, within the bound.
A program may use at most 128 MiB of HBM per device.

```python
import math
import jax
import jax.numpy as jnp
from jax import lax

D = 4096
QUERY_HEADS = 16
KEY_VALUE_HEADS = 4
HEAD_SIZE = 128
SEQUENCE_TOKENS = 2048
RELAY_SECTIONS = 4


def draw_pairs(key):
    folded = jax.random.fold_in(key, 11)
    random_query_split, random_key_split = jax.random.split(folded, 2)
    query_group_size = QUERY_HEADS // KEY_VALUE_HEADS
    random_rows_split = jnp.clip(jax.random.normal(random_key_split, (RELAY_SECTIONS, SEQUENCE_TOKENS, KEY_VALUE_HEADS, HEAD_SIZE), jnp.float32), -6.0, 6.0)
    rows_of_queries = 2.0 * jnp.clip(jax.random.normal(random_query_split, (RELAY_SECTIONS, SEQUENCE_TOKENS, KEY_VALUE_HEADS, query_group_size, HEAD_SIZE), jnp.float32), -6.0, 6.0)
    return (rows_of_queries.reshape(RELAY_SECTIONS, SEQUENCE_TOKENS, QUERY_HEADS * HEAD_SIZE), random_rows_split.reshape(RELAY_SECTIONS, SEQUENCE_TOKENS, KEY_VALUE_HEADS * HEAD_SIZE))


def draw_queries(key, part):
    return draw_pairs(key)[0].astype(jnp.bfloat16)


def draw_keys(key, part):
    return draw_pairs(key)[1].astype(jnp.bfloat16)


def block_levels(own_key, shape, pieces, smallest, largest):
    gain, own = 1.0, jax.random.fold_in(own_key, 6)
    for axis_at, blocks in pieces:
        steps = jnp.exp(jax.random.uniform(jax.random.fold_in(own, axis_at), (blocks,), jnp.float32, smallest / len(pieces), largest / len(pieces)))
        gain = gain * jnp.repeat(steps, shape[axis_at] // blocks).reshape([-1 if axis == axis_at else 1 for axis in range(len(shape))])
    return gain


def gaussian(stream_key, extent, width, limit, cuts=(), held_as=jnp.bfloat16):
    gain = block_levels(stream_key, extent, cuts, -0.22, 0.18) if cuts else 1.0
    array = jax.random.normal(stream_key, extent, jnp.float32) * width * gain
    return jnp.minimum(jnp.maximum(array, -limit), limit).astype(held_as)


def setup_inputs(seed: int = 0) -> dict:
    splits = jax.random.split(jax.random.key(seed), 5)
    return {
        "queries": draw_queries(jax.random.fold_in(splits[4], 71), 0),
        "keys": draw_keys(jax.random.fold_in(splits[4], 71), 0),
        "values": gaussian(splits[2], (RELAY_SECTIONS, SEQUENCE_TOKENS, KEY_VALUE_HEADS * HEAD_SIZE), 4.0, 24.0, ((0, 4), (1, 8))),
        "out_weight": gaussian(splits[3], (RELAY_SECTIONS, QUERY_HEADS * HEAD_SIZE, D), (QUERY_HEADS * HEAD_SIZE) ** -0.5, 0.125, ((0, 4),)),
    }


def attend_section(operands):
    queries, keys, values, out_weight = operands
    query_group_size = QUERY_HEADS // KEY_VALUE_HEADS
    heads_of_queries = queries.reshape(SEQUENCE_TOKENS, KEY_VALUE_HEADS, query_group_size, HEAD_SIZE).astype(jnp.float32)
    heads_of_keys = keys.reshape(SEQUENCE_TOKENS, KEY_VALUE_HEADS, HEAD_SIZE).astype(jnp.float32)
    heads_of_values = values.reshape(SEQUENCE_TOKENS, KEY_VALUE_HEADS, HEAD_SIZE).astype(jnp.float32)
    block_len = min(SEQUENCE_TOKENS, 1024)
    scale = 1.0 / math.sqrt(HEAD_SIZE)
    pieces_out = []
    for block_id in range(SEQUENCE_TOKENS // block_len):
        finish = (block_id + 1) * block_len
        scores = jnp.einsum('rhgd,khd->hgrk', heads_of_queries[block_id * block_len:finish], heads_of_keys[:finish]) * scale
        query_positions = block_id * block_len + jnp.arange(block_len)
        visible = jnp.arange(finish)[None, :] <= query_positions[:, None]
        scores = jnp.where(visible, scores, -jnp.inf)
        highest = lax.optimization_barrier(jnp.max(scores, axis=-1, keepdims=True))
        weights = jnp.exp(scores - highest).astype(jnp.bfloat16)
        totals = lax.optimization_barrier(jnp.sum(weights.astype(jnp.float32), axis=-1))
        summed = jnp.einsum('hgrk,khd->hgrd', weights.astype(jnp.float32), heads_of_values[:finish])
        result = summed / totals[..., None]
        pieces_out.append(jnp.transpose(result, (2, 0, 1, 3)).reshape(block_len, QUERY_HEADS * HEAD_SIZE).astype(jnp.bfloat16))
    attended = jnp.concatenate(pieces_out, axis=0)
    return jnp.dot(attended, out_weight, preferred_element_type=jnp.float32).astype(jnp.bfloat16)

def reference(queries, keys, values, out_weight):
    section_out = lax.map(attend_section, (queries, keys, values, out_weight))
    return jnp.roll(section_out, 1, axis=0)
```

```python
import functools
import math

import jax
import jax.numpy as jnp
from jax import lax
from jax.experimental import pallas as pl
from jax.experimental.pallas import tpu as pltpu
from jax.sharding import PartitionSpec as P

HEAD_SIZE = 128
COLUMNS = 256
PARTS = 4
AHEAD = 2
MOVED = (1, 3)
EXTRA = 16
VMEM_LIMIT = 50 * 1024 * 1024
MESH = pl.DeviceIdType.MESH


def kernel(sections, spans, across, q_ref, k_ref, v_ref, w_ref, o_ref, held, weight, stacked, acc, top,
           attended, projected, pair_send, pair_recv, far_send, pass_send, relay_send, span_recv, weight_sem, out_send, out_recv,
           own_sem, query_sem, aside, aside_recv, cross_send):
    rows, kv_width = k_ref.shape
    q_width = q_ref.shape[1]
    heads = kv_width // HEAD_SIZE
    group = q_width // kv_width
    chips = spans // 2
    pieces = weight.shape[0]
    section = lax.axis_index("pipe")
    me = lax.axis_index("ctx")
    chip, core = me // 2, lax.rem(me, 2)
    line, column = chip // across, lax.rem(chip, across)
    lines = chips // across
    following = lax.rem(section + 1, sections)
    before = lax.rem(section + sections - 1, sections)
    factor = math.log2(math.e) / math.sqrt(HEAD_SIZE)

    barrier = pltpu.get_barrier_semaphore()

    @pl.loop(1, spans)
    def _(step):
        pl.semaphore_signal(barrier, inc=1, device_id={"ctx": lax.rem(me + step, spans)}, device_id_type=MESH)

    @pl.loop(0, chips)
    def _(other):
        pl.semaphore_signal(
            barrier, inc=1, device_id={"pipe": before, "ctx": other * 2 + core}, device_id_type=MESH)

    def weight_copy(piece):
        return pltpu.make_async_copy(
            w_ref.at[:, pl.ds(pl.multiple_of(piece * COLUMNS, COLUMNS), COLUMNS)],
            weight.at[piece], weight_sem.at[piece])

    part_width = kv_width // PARTS

    def place(owner, side, which, part):
        return held.at[owner, which, part, pl.ds(pl.multiple_of(side * rows, rows), rows), :]

    def own_copy(which, part):
        return pltpu.make_async_copy(
            (k_ref, v_ref)[which].at[:, part * part_width:(part + 1) * part_width],
            place(chip, core, which, part), own_sem.at[which, part])

    def each_part(act):
        for part in range(PARTS):
            for which in range(2):
                act(which, part)

    def query_copy(head, member):
        at = head * group + member
        return pltpu.make_async_copy(
            q_ref.at[:, at * HEAD_SIZE:(at + 1) * HEAD_SIZE],
            stacked.at[head, member * rows:(member + 1) * rows, :], query_sem.at[at])

    each_part(lambda *at: own_copy(*at).start())
    for head in range(heads):
        for member in range(group):
            query_copy(head, member).start()

    @pl.loop(0, pieces)
    def _(piece):
        weight_copy(piece).start()

    each_part(lambda *at: own_copy(*at).wait())

    def pair_copy(which, part):
        return pltpu.make_async_remote_copy(
            place(chip, core, which, part), place(chip, core, which, part), pair_send.at[which, part],
            pair_recv.at[which, part], device_id={"ctx": chip * 2 + 1 - core}, device_id_type=MESH)

    def far_copy(target, which, part):
        return pltpu.make_async_remote_copy(
            place(chip, core, which, part), place(chip, core, which, part), far_send.at[target, which, part],
            span_recv.at[chip, core, which, part], device_id={"ctx": target * 2 + core}, device_id_type=MESH)

    def pass_copy(owner, which, part):
        return pltpu.make_async_remote_copy(
            place(owner, core, which, part), place(owner, core, which, part), pass_send.at[owner, which, part],
            span_recv.at[owner, core, which, part], device_id={"ctx": chip * 2 + 1 - core}, device_id_type=MESH)

    def relay_copy(owner, target, at, which, part):
        return pltpu.make_async_remote_copy(
            place(owner, core, which, part), place(owner, core, which, part), relay_send.at[owner, at, which, part],
            span_recv.at[owner, core, which, part], device_id={"ctx": target * 2 + core}, device_id_type=MESH)

    def each_own(part, act):
        @pl.loop(column + 1, across)
        def _(other):
            act(line * across + other, 0, part)
            act(line * across + other, 1, part)

        @pl.loop(line + 1, lines)
        def _(other):
            act(other * across + column, 1, part)
            act(other * across + column, 0, part)

    def each_relay(owner, which, part, act):
        beside = owner // across == line
        above = jnp.logical_not(beside) & (lax.rem(owner, across) == column)
        if which == 0:
            @pl.when(beside)
            def _():
                @pl.loop(line + 1, lines)
                def _(other):
                    act(owner, other * across + column, other, which, part)

            @pl.when(above)
            def _():
                @pl.loop(0, column)
                def _(other):
                    act(owner, line * across + other, other, which, part)
        else:
            @pl.when(above)
            def _():
                @pl.loop(1, across)
                def _(step):
                    other = lax.rem(column + step, across)
                    act(owner, line * across + other, other, which, part)

    def wait_span(owner, side, which, part):
        pltpu.make_async_remote_copy(
            place(owner, side, which, part), place(owner, side, which, part), pass_send.at[owner, which, part],
            span_recv.at[owner, side, which, part], device_id={"ctx": chip * 2 + 1 - core},
            device_id_type=MESH).wait_recv()

    pl.semaphore_wait(barrier, spans - 1 + chips)
    each_part(lambda *at: pair_copy(*at).start())

    for part in range(PARTS):
        each_own(part, lambda *at: far_copy(*at).start())

    for head in range(heads):
        for member in range(group):
            query_copy(head, member).wait()

    def block(owner, part, within, first):
        head = part * (heads // PARTS) + within
        lanes = slice(within * HEAD_SIZE, (within + 1) * HEAD_SIZE)
        scores = lax.dot_general(
            held[owner, 0, part, :, lanes], stacked[head], (((1,), (1,)), ((), ())),
            preferred_element_type=jnp.float32)
        if first:
            key = lax.broadcasted_iota(jnp.int32, scores.shape, 0)
            row = lax.rem(lax.broadcasted_iota(jnp.int32, scores.shape, 1), rows) + core * rows
            scores = jnp.where(key <= row, scores, -1e30)
        highest = jnp.max(scores, axis=0, keepdims=True)
        if not first:
            previous = top[head]
            highest = jnp.maximum(previous, highest)
            rescale = jnp.exp2((previous - highest) * factor)
        top[head] = highest
        weights = jnp.exp2((scores - highest) * factor).astype(jnp.bfloat16)
        values = held[owner, 1, part, :, lanes].T
        values = jnp.concatenate([values, jnp.ones((EXTRA, values.shape[1]), values.dtype)], axis=0)
        summed = jnp.dot(values, weights, preferred_element_type=jnp.float32)
        if first:
            acc[head] = summed
        else:
            acc[head] = acc[head] * rescale + summed

    for part in range(PARTS):
        for which in range(2):
            pair_copy(which, part).wait_recv()
        for within in range(heads // PARTS):
            block(chip, part, within, True)

    near = line + column
    apart = line * (across - 1)

    def source(step):
        early = step < near * PARTS
        count = jnp.maximum(jnp.where(early, near, apart), 1)
        order = jnp.where(early, step, step - near * PARTS)
        part = order // count
        nth = order - part * count
        others = max(across - 1, 1)
        direct = jnp.where(
            nth < column, line * across + column - 1 - nth, (line - 1 - nth + column) * across + column)
        relayed = (line - 1 - nth // others) * across + lax.rem(column + 1 + lax.rem(nth, others), across)
        return jnp.where(early, direct, relayed), part

    @pl.loop(0, jnp.where(chip > 0, chip * PARTS + AHEAD, 0))
    def _(step):
        @pl.when(step < chip * PARTS)
        def _():
            owner, part = source(step)
            for which in range(2):
                wait_span(owner, core, which, part)
                each_relay(owner, which, part, lambda *at: relay_copy(*at).start())
                pass_copy(owner, which, part).start()

        @pl.when(step >= AHEAD)
        def _():
            owner, part = source(step - AHEAD)
            for which in range(2):
                wait_span(owner, 1 - core, which, part)
            for within in range(heads // PARTS):
                block(owner, part, within, False)

    for head in range(heads):
        for member in range(group):
            share = acc[head, :, member * rows:(member + 1) * rows]
            attended[:, (head * group + member) * HEAD_SIZE:(head * group + member + 1) * HEAD_SIZE] = (
                share[:HEAD_SIZE] / share[HEAD_SIZE:HEAD_SIZE + 1]).T.astype(jnp.bfloat16)

    def out_copy(piece):
        return pltpu.make_async_remote_copy(
            projected.at[piece],
            o_ref.at[:, pl.ds(pl.multiple_of(piece * COLUMNS, COLUMNS), COLUMNS)],
            out_send.at[piece], out_recv.at[piece], device_id={"pipe": following}, device_id_type=MESH)

    late = chips - chips // 2
    slot_of = lax.rem(chip + 2 * chips - late, 2)
    moved = jnp.where(chip >= late, jnp.where(slot_of == 0, MOVED[0], MOVED[1]), 0)

    def aside_copy(piece):
        return pltpu.make_async_remote_copy(
            projected.at[piece], aside.at[slot_of, piece], out_send.at[piece],
            aside_recv.at[slot_of, piece],
            device_id={"ctx": (chip - late) // 2 * 2 + core}, device_id_type=MESH)

    def cross_copy(slot, piece):
        return pltpu.make_async_remote_copy(
            aside.at[slot, piece],
            o_ref.at[:, pl.ds(pl.multiple_of(piece * COLUMNS, COLUMNS), COLUMNS)],
            cross_send.at[slot, piece], out_recv.at[piece],
            device_id={"pipe": following, "ctx": (late + chip * 2 + slot) * 2 + core}, device_id_type=MESH)

    def each_carried(act):
        for slot in range(2):
            @pl.when(late + chip * 2 + slot < chips)
            def _():
                @pl.loop(0, MOVED[slot])
                def _(piece):
                    act(slot, piece)

    def carry(slot, piece):
        pltpu.make_async_remote_copy(
            aside.at[slot, piece], aside.at[slot, piece], cross_send.at[slot, piece],
            aside_recv.at[slot, piece], device_id={"pipe": following}, device_id_type=MESH).wait_recv()
        cross_copy(slot, piece).start()

    @pl.loop(0, pieces)
    def _(piece):
        weight_copy(piece).wait()
        projected[piece] = jnp.dot(
            attended[...], weight[piece], preferred_element_type=jnp.float32).astype(jnp.bfloat16)

        @pl.when(piece < moved)
        def _():
            aside_copy(piece).start()

        @pl.when(piece >= moved)
        def _():
            out_copy(piece).start()

    each_carried(carry)

    each_part(lambda *at: pair_copy(*at).wait_send())

    for part in range(PARTS):
        each_own(part, lambda *at: far_copy(*at).wait_send())

    @pl.loop(0, chip)
    def _(owner):
        for part in range(PARTS):
            for which in range(2):
                each_relay(owner, which, part, lambda *at: relay_copy(*at).wait_send())
                pass_copy(owner, which, part).wait_send()

    each_carried(lambda *at: cross_copy(*at).wait_send())

    @pl.loop(0, pieces)
    def _(piece):
        out_copy(piece).wait()


def per_device(sections, spans, queries, keys, values, out_weight):
    rows, q_width = queries.shape[1:]
    kv_width = keys.shape[2]
    width = out_weight.shape[2]
    heads = kv_width // HEAD_SIZE
    stack = q_width // kv_width * rows
    pieces = width // COLUMNS
    chips = spans // 2
    across = math.isqrt(chips)
    across = across if chips % across == 0 else chips
    hbm = pl.BlockSpec(memory_space=pltpu.HBM)
    handed = pl.pallas_call(
        functools.partial(kernel, sections, spans, across),
        out_shape=jax.ShapeDtypeStruct((rows, width), jnp.bfloat16),
        in_specs=[hbm] * 4,
        out_specs=pl.BlockSpec(memory_space=pl.ANY),
        scratch_shapes=[
            pltpu.VMEM((chips, 2, PARTS, 2 * rows, kv_width // PARTS), jnp.bfloat16),
            pltpu.VMEM((pieces, q_width, COLUMNS), jnp.bfloat16),
            pltpu.VMEM((heads, stack, HEAD_SIZE), jnp.bfloat16),
            pltpu.VMEM((heads, HEAD_SIZE + EXTRA, stack), jnp.float32),
            pltpu.VMEM((heads, 1, stack), jnp.float32),
            pltpu.VMEM((rows, q_width), jnp.bfloat16),
            pltpu.VMEM((pieces, rows, COLUMNS), jnp.bfloat16),
            pltpu.SemaphoreType.DMA((2, PARTS)),
            pltpu.SemaphoreType.DMA((2, PARTS)),
            pltpu.SemaphoreType.DMA((chips, 2, PARTS)),
            pltpu.SemaphoreType.DMA((chips, 2, PARTS)),
            pltpu.SemaphoreType.DMA((chips, max(across, chips // across), 2, PARTS)),
            pltpu.SemaphoreType.DMA((chips, 2, 2, PARTS)),
            pltpu.SemaphoreType.DMA((pieces,)),
            pltpu.SemaphoreType.DMA((pieces,)),
            pltpu.SemaphoreType.DMA((pieces,)),
            pltpu.SemaphoreType.DMA((2, PARTS)),
            pltpu.SemaphoreType.DMA((q_width // HEAD_SIZE,)),
            pltpu.VMEM((2, max(MOVED), rows, COLUMNS), jnp.bfloat16),
            pltpu.SemaphoreType.DMA((2, max(MOVED))),
            pltpu.SemaphoreType.DMA((2, max(MOVED))),
        ],
        compiler_params=pltpu.CompilerParams(
            collective_id=0, has_side_effects=True, vmem_limit_bytes=VMEM_LIMIT),
    )(*(pltpu.with_memory_space_constraint(each[0], pltpu.HBM) for each in (queries, keys, values, out_weight)))
    return handed[None]


def solution(mesh):
    placed = (
        P("pipe", "ctx", None),
        P("pipe", "ctx", None),
        P("pipe", "ctx", None),
        P("pipe", None, None),
    )
    return jax.shard_map(
        functools.partial(per_device, mesh.shape["pipe"], mesh.shape["ctx"]),
        mesh=mesh, in_specs=placed, out_specs=P("pipe", "ctx", None), check_vma=False
    )
```
